32 devices in a mesh: batch: 8 (over y, x, core), chan: 4 (over z).
Axes of the slice: x: 2, y: 2, z: 4, core: 2. Of those that a mesh axis runs over, the one named last changes fastest.
Arguments:
- fine_inputs: bfloat16 [8, 32, 32, 512], P('batch'), may hold values from -6 to 6
- fine_upstream: bfloat16 [8, 32, 32, 512], P('batch', None, None, 'chan'), may hold values from -6 to 6
- fine_bank: bfloat16 [8, 9, 512, 512], P(None, None, 'batch', 'chan'), may hold values from -0.09375 to 0.09375
- fine_coefs: float32 [8, 8], replicated, may hold values from 0 to 1, as said below
- coarse_inputs: bfloat16 [8, 16, 16, 512], P('batch'), may hold values from -6 to 6
- coarse_upstream: bfloat16 [8, 16, 16, 512], P('batch', None, None, 'chan'), may hold values from -6 to 6
- coarse_bank: bfloat16 [8, 9, 512, 512], P(None, None, 'batch', 'chan'), may hold values from -0.09375 to 0.09375
- coarse_coefs: float32 [8, 8], replicated, may hold values from 0 to 1, as said below
Outputs:
- fine_delta: bfloat16 [8, 32, 32, 512], P('batch', None, None, 'chan')
- fine_update: float32 [8, 9, 512, 512], P(None, None, 'batch', 'chan')
- fine_logit: float32 [8, 8], P('batch')
- coarse_delta: bfloat16 [8, 16, 16, 512], P('batch', None, None, 'chan')
- coarse_update: float32 [8, 9, 512, 512], P(None, None, 'batch', 'chan')
- coarse_logit: float32 [8, 8], P('batch')
The draws below stay inside these ranges and needn't reach their ends.
Inputs may be any that keep to these rules, and one draw needn't show every extreme that they name: Each row of fine_coefs is a softmax: positive entries that sum to one. Each row of coarse_coefs is a softmax: positive entries that sum to one.
All inputs are finite; a program needn't handle non-finite values.
Results may differ from the reference program's by a relative error of at most 0.01.
Values may be sent and summed in bfloat16 or wider, within the bound.
No kernel may reach another device: no remote copies, remote signals or barrier semaphores. Data moves between devices by JAX's collectives and lax.ppermute only.
A program may use at most 128 MiB of HBM per device.

```python
import jax
import jax.numpy as jnp
from jax import lax

CHANNELS_IN = 512
CHANNELS_OUT = 512
BANKS = 8
FINE_SIDE = 32
COARSE_SIDE = 16
SAMPLES = 8
N_CHAN = 4


def softmax_rows(key, salt):
    sub = jax.random.fold_in(key, salt)
    logits = 1.5 * jax.random.normal(sub, (SAMPLES, BANKS), jnp.float32)
    return jax.nn.softmax(logits, axis=1).astype(jnp.float32)


def draw_fine_coefs(key, part):
    return softmax_rows(key, 11)


def draw_coarse_coefs(key, part):
    return softmax_rows(key, 23)


def block_levels(rng, shape, split, low, largest):
    factor_of, own = 1.0, jax.random.fold_in(rng, 6)
    for axis_at, parts in split:
        heights = jnp.exp(jax.random.uniform(jax.random.fold_in(own, axis_at), (parts,), jnp.float32, low / len(split), largest / len(split)))
        factor_of = factor_of * jnp.repeat(heights, shape[axis_at] // parts).reshape([-1 if axis == axis_at else 1 for axis in range(len(shape))])
    return factor_of


def bell_draw(stream_key, shape, spread, limit, cuts=(), kind=jnp.bfloat16):
    result = jax.random.normal(stream_key, shape, jnp.float32) * spread
    if len(cuts) > 0:
        result = block_levels(stream_key, shape, cuts, -0.22, 0.18) * result
    return jnp.clip(result, min=-limit, max=limit).astype(kind)


def setup_inputs(seed: int = 0) -> dict:
    streams_of = jax.random.split(jax.random.key(seed), 9)
    return {
        "fine_inputs": bell_draw(streams_of[0], (SAMPLES, FINE_SIDE, FINE_SIDE, CHANNELS_IN), 1.0, 6.0, ((0, 8),)),
        "fine_upstream": bell_draw(streams_of[1], (SAMPLES, FINE_SIDE, FINE_SIDE, CHANNELS_OUT), 1.0, 6.0, ((0, 8), (3, 4))),
        "fine_bank": bell_draw(streams_of[2], (BANKS, 9, CHANNELS_IN, CHANNELS_OUT), (9 * CHANNELS_IN) ** -0.5, 0.09375, ((2, 8), (3, 4))),
        "fine_coefs": draw_fine_coefs(jax.random.fold_in(streams_of[8], 71), 0),
        "coarse_inputs": bell_draw(streams_of[4], (SAMPLES, COARSE_SIDE, COARSE_SIDE, CHANNELS_IN), 1.0, 6.0, ((0, 8),)),
        "coarse_upstream": bell_draw(streams_of[5], (SAMPLES, COARSE_SIDE, COARSE_SIDE, CHANNELS_OUT), 1.0, 6.0, ((0, 8), (3, 4))),
        "coarse_bank": bell_draw(streams_of[6], (BANKS, 9, CHANNELS_IN, CHANNELS_OUT), (9 * CHANNELS_IN) ** -0.5, 0.09375, ((2, 8), (3, 4))),
        "coarse_coefs": draw_coarse_coefs(jax.random.fold_in(streams_of[8], 71), 0),
    }


HIGH = lax.Precision.HIGHEST


def mix_kernels(coefs, bank_all):
    flat = bank_all.reshape(bank_all.shape[0], -1).astype(jnp.float32)
    mixed = jnp.dot(coefs, flat, precision=HIGH)
    return mixed.reshape((coefs.shape[0],) + bank_all.shape[1:]).astype(jnp.bfloat16)


def sample_backward(inputs, upstream, kernel, side):
    padded_in = jnp.pad(inputs, ((1, 1), (1, 1), (0, 0))).astype(jnp.float32)
    padded_up = jnp.pad(upstream, ((1, 1), (1, 1), (0, 0))).astype(jnp.float32)
    flat_up = upstream.astype(jnp.float32).reshape(side * side, -1)
    kernel_f = kernel.astype(jnp.float32)
    group = CHANNELS_OUT // N_CHAN
    grad_taps = []
    windows_up = []
    for row_shift in range(3):
        for col_shift in range(3):
            window_in = padded_in[row_shift:row_shift + side, col_shift:col_shift + side, :].reshape(side * side, -1)
            grad_taps.append(jnp.dot(window_in.T, flat_up, precision=HIGH) / side)
            windows_up.append(padded_up[2 - row_shift:2 - row_shift + side, 2 - col_shift:2 - col_shift + side, :].reshape(side * side, -1))
    delta = jnp.zeros((side * side, CHANNELS_IN), jnp.float32)
    for which in range(N_CHAN):
        partial_sum = jnp.zeros((side * side, CHANNELS_IN), jnp.float32)
        for tap in range(9):
            cols = windows_up[tap][:, which * group:(which + 1) * group]
            weights = kernel_f[tap][:, which * group:(which + 1) * group]
            partial_sum = partial_sum + jnp.dot(cols, weights.T, precision=HIGH)
        delta = delta + partial_sum.astype(jnp.bfloat16).astype(jnp.float32)
    return delta.astype(jnp.bfloat16).reshape(side, side, CHANNELS_IN), jnp.stack(grad_taps, axis=0)


def layer_backward(inputs, upstream, bank_all, coefs, side):
    kernels = mix_kernels(coefs, bank_all)
    flat_bank = bank_all.reshape(BANKS, -1).astype(jnp.float32)

    def step(total, items):
        x_in, g_up, kern, coef_row = items
        delta, grad = sample_backward(x_in, g_up, kern, side)
        flat_grad = grad.reshape(-1)
        dcoef = jnp.dot(flat_bank, flat_grad, precision=HIGH)
        total = total + coef_row[:, None] * flat_grad[None, :]
        return total, (delta, dcoef)

    start = jnp.zeros((BANKS, 9 * CHANNELS_IN * CHANNELS_OUT), jnp.float32)
    total, (deltas, dcoefs) = lax.scan(step, start, (inputs, upstream, kernels, coefs))
    logit = coefs * (dcoefs - jnp.sum(coefs * dcoefs, axis=1, keepdims=True))
    return deltas, total.reshape(bank_all.shape), logit


def reference(fine_inputs, fine_upstream, fine_bank, fine_coefs, coarse_inputs, coarse_upstream, coarse_bank, coarse_coefs):
    fine_delta, fine_update, fine_logit = layer_backward(fine_inputs, fine_upstream, fine_bank, fine_coefs, FINE_SIDE)
    coarse_delta, coarse_update, coarse_logit = layer_backward(coarse_inputs, coarse_upstream, coarse_bank, coarse_coefs, COARSE_SIDE)
    return (fine_delta, fine_update, fine_logit, coarse_delta, coarse_update, coarse_logit)
```

```python
import functools

import jax
import jax.numpy as jnp
from jax import lax
from jax.experimental import pallas as pl
from jax.experimental.pallas import tpu as pltpu
from jax.sharding import PartitionSpec as P

HIGH = lax.Precision.HIGHEST
F32 = jnp.float32
BF16 = jnp.bfloat16
TAPS = 9


def shifted(padded, row_shift, col_shift, side):
    window = padded[:, row_shift : row_shift + side, col_shift : col_shift + side, :]
    return window.reshape(window.shape[0], side * side, window.shape[3])


def local_grads(inputs, upstream, kernels, side):
    samples_here = inputs.shape[0]
    pad_in = jnp.pad(inputs, ((0, 0), (1, 1), (1, 1), (0, 0)))
    pad_up = jnp.pad(upstream, ((0, 0), (1, 1), (1, 1), (0, 0)))
    flat_up = upstream.reshape(samples_here, side * side, upstream.shape[3])
    delta = jnp.zeros((samples_here, side * side, inputs.shape[3]), F32)
    grad_taps = []
    for row_shift in range(3):
        for col_shift in range(3):
            tap = 3 * row_shift + col_shift
            window_in = shifted(pad_in, row_shift, col_shift, side)
            window_up = shifted(pad_up, 2 - row_shift, 2 - col_shift, side)
            grad_taps.append(
                jnp.einsum("bpc,bpo->bco", window_in, flat_up, preferred_element_type=F32) / side
            )
            delta = delta + jnp.einsum(
                "bpo,bco->bpc", window_up, kernels[:, tap], preferred_element_type=F32
            )
    return (delta.reshape(samples_here, side, side, inputs.shape[3]), jnp.stack(grad_taps, axis=1))


def plain_layer(inputs, upstream, bank_part, coefs):
    side = inputs.shape[1]
    flat_bank = bank_part.reshape(bank_part.shape[0], -1).astype(F32)
    mixed_all = jnp.dot(coefs, flat_bank, precision=HIGH)
    mixed_all = mixed_all.reshape((coefs.shape[0],) + bank_part.shape[1:]).astype(BF16)
    kernels = lax.all_to_all(mixed_all, "batch", split_axis=0, concat_axis=2, tiled=True)
    delta, kernel_grad = local_grads(inputs, upstream, kernels, side)
    delta_total = lax.psum(delta.astype(BF16), "chan").astype(F32)
    width = delta.shape[3] // lax.axis_size("chan")
    delta_part = lax.dynamic_slice_in_dim(delta_total, lax.axis_index("chan") * width, width, 3)
    moved = lax.all_to_all(
        kernel_grad.astype(BF16), "batch", split_axis=2, concat_axis=0, tiled=True
    ).astype(kernel_grad.dtype)
    flat_grads = moved.reshape(moved.shape[0], -1)
    update = jnp.dot(coefs.T, flat_grads, precision=HIGH).reshape(bank_part.shape)
    dcoef_part = lax.dot_general(flat_grads, flat_bank, (((1,), (1,)), ((), ())), precision=HIGH)
    return (delta_part.astype(BF16), update, dcoef_part)


def plain_logits(coefs, totals, samples_here):
    first_row = lax.axis_index("batch") * samples_here
    own_coefs = lax.dynamic_slice_in_dim(coefs, first_row, samples_here, 0)
    own_totals = lax.dynamic_slice_in_dim(totals, first_row, samples_here, 0)
    return own_coefs * (own_totals - jnp.sum(own_coefs * own_totals, axis=1, keepdims=True))


def plain_device(fi, fu, fb, fc, ci, cu, cb, cc):
    fine_delta, fine_update, fine_partial = plain_layer(fi, fu, fb, fc)
    coarse_delta, coarse_update, coarse_partial = plain_layer(ci, cu, cb, cc)
    fine_total, coarse_total = lax.psum((fine_partial, coarse_partial), ("batch", "chan"))
    fine_logit = plain_logits(fc, fine_total, fi.shape[0])
    coarse_logit = plain_logits(cc, coarse_total, fi.shape[0])
    return (fine_delta, fine_update, fine_logit, coarse_delta, coarse_update, coarse_logit)


def place():
    me = lax.axis_index("batch")
    return me, lax.div(me, 2), lax.rem(me, 2), lax.axis_index("chan")


def vmem(n):
    return [pl.BlockSpec(memory_space=pltpu.VMEM) for _ in range(n)]


def smem(n):
    return [pl.BlockSpec(memory_space=pltpu.SMEM) for _ in range(n)]


def call(body, out_shapes, n_smem, n_vmem, scratch=(), flops=0, nbytes=0, name=None):
    return pl.pallas_call(
        body,
        out_shape=out_shapes,
        in_specs=smem(n_smem) + vmem(n_vmem),
        out_specs=jax.tree.map(lambda _: pl.BlockSpec(memory_space=pltpu.VMEM), out_shapes),
        scratch_shapes=list(scratch),
        cost_estimate=pl.CostEstimate(flops=flops, bytes_accessed=nbytes, transcendentals=0),
        name=name,
    )


def make_windows(up, side, windows_ref):
    pixels, width = up.shape
    wide = up.astype(F32)
    col = lax.rem(lax.broadcasted_iota(jnp.int32, (pixels, width), 0), side)
    by_col = (
        jnp.where(col == side - 1, 0.0, pltpu.roll(wide, pixels - 1, 0)).astype(BF16),
        up,
        jnp.where(col == 0, 0.0, pltpu.roll(wide, 1, 0)).astype(BF16),
    )
    zeros = jnp.zeros((side, width), BF16)
    for dx in range(3):
        view = by_col[dx]
        top, mid, low = (slice(k * width, (k + 1) * width) for k in (dx, 3 + dx, 6 + dx))
        windows_ref[0 : pixels - side, top] = view[side:]
        windows_ref[pixels - side :, top] = zeros
        windows_ref[:, mid] = view
        windows_ref[0:side, low] = zeros
        windows_ref[side:, low] = view[: pixels - side]


def mix_rows(coefs, row, bank, out, offset):
    banks, taps, rows, width = bank.shape
    weights = [coefs[row, k] for k in range(banks)]

    def step(t, carry):
        total = weights[0] * bank[0, t].astype(F32)
        for k in range(1, banks):
            total = total + weights[k] * bank[k, t].astype(F32)
        lanes = pl.ds(pl.multiple_of(t * width, width), width)
        out[pl.ds(offset, rows), lanes] = total.astype(BF16)
        return carry

    lax.fori_loop(0, taps, step, 0)


def mix_pair(coefs, own, other, outs):
    me, _, half, _ = place()
    rows = own.shape[2]
    for d, out in enumerate(outs):
        row = jnp.bitwise_xor(me, 2 * d)
        mix_rows(coefs, row, own, out, pl.multiple_of(half * rows, rows))
        mix_rows(coefs, row, other, out, pl.multiple_of((1 - half) * rows, rows))


def dot_nt(a, b):
    return lax.dot_general(a, b, (((1,), (1,)), ((), ())), preferred_element_type=F32)


def dot_tn(a, b):
    return lax.dot_general(a, b, (((0,), (0,)), ((), ())), preferred_element_type=F32)


def mix_body(pairs, coefs, own, other, *outs):
    mix_pair(coefs, own, other, outs)


def pack_body(pairs, inputs, up, *outs):
    _, pair, _, _ = place()
    pixels, width = up.shape
    for d, out in enumerate(outs):
        out[0:pixels, :] = up[...]
        first = pl.multiple_of(jnp.bitwise_xor(pair, d) * width, width)
        out[pixels:, :] = inputs[:, pl.ds(first, width)]


def grads_body(pairs, side, inputs, up, *rest):
    outs, (windows, grads) = rest[:pairs], rest[pairs:]
    _, pair, _, _ = place()
    make_windows(up[...], side, windows)
    third = windows.shape[1] // 3
    x = inputs[...]
    for part in range(3):
        lanes = slice(part * third, (part + 1) * third)
        grads[:, lanes] = (dot_tn(x, windows[:, lanes]) * (1.0 / side)).astype(BF16)
    rows = grads.shape[0] // pairs
    for d, out in enumerate(outs):
        first = pl.multiple_of(jnp.bitwise_xor(pair, d) * rows, rows)
        out[...] = grads[pl.ds(first, rows), :]


def delta_body(pairs, side, up, *rest):
    mixed, outs, (windows, kernels) = rest[:pairs], rest[pairs : 2 * pairs], rest[2 * pairs :]
    _, pair, _, chan = place()
    rows = kernels.shape[0] // pairs
    for d in range(pairs):
        slot = jnp.bitwise_xor(jnp.bitwise_xor(pair, d), chan)
        kernels[pl.ds(pl.multiple_of(slot * rows, rows), rows), :] = mixed[d][...]
    make_windows(up[...], side, windows)
    win = windows[...]
    step = 2 if pairs % 2 == 0 else 1
    for slot in range(0, pairs, step):
        both = dot_nt(win, kernels[slot * rows : (slot + step) * rows, :])
        for k in range(step):
            outs[slot + k][...] = both[:, k * rows : (k + 1) * rows].astype(BF16)


def coarse_body(pairs, side, coefs, own, other, *rest):
    bufs, parts, grads = rest[:pairs], rest[pairs : 2 * pairs], rest[2 * pairs : 3 * pairs]
    windows, staged = rest[3 * pairs : 3 * pairs + 2]
    mixed = rest[3 * pairs + 2 :]
    _, pair, _, chan = place()
    mix_pair(coefs, own, other, mixed)
    pixels = side * side
    for d in range(pairs):
        make_windows(bufs[d][0:pixels, :], side, windows)
        win = windows[...]
        slot = jnp.bitwise_xor(jnp.bitwise_xor(pair, d), chan)
        staged[slot] = dot_nt(win, mixed[d][...]).astype(BF16)
        grads[d][...] = (dot_tn(bufs[d][pixels:, :], win) * (1.0 / side)).astype(BF16)
    for d in range(pairs):
        parts[d][...] = staged[d]


def update_body(pairs, lane0, has_more, coefs, bank, *rest):
    gots = rest[: 2 * pairs]
    rest = rest[2 * pairs :]
    more = rest[0] if has_more else None
    rest = rest[1:] if has_more else rest
    update, dcoef, all_grads, all_bank = rest
    me, _, half, _ = place()
    banks, taps, rows, width = bank.shape
    samples = 2 * pairs
    for d in range(pairs):
        for r in range(2):
            first = pl.multiple_of(half * rows, rows)
            at = (2 * d + r) * rows
            all_grads[at : at + rows, :] = gots[r * pairs + d][pl.ds(first, rows), :]
    for k in range(banks):
        for t in range(taps):
            all_bank[k * rows : (k + 1) * rows, t * width : (t + 1) * width] = bank[k, t]
    cross = dot_nt(all_grads[...], all_bank[...])
    shape = cross.shape
    row = lax.rem(lax.broadcasted_iota(jnp.int32, shape, 0), rows)
    col = lax.rem(lax.broadcasted_iota(jnp.int32, shape, 1), rows)
    kept = jnp.where(row == col, cross, 0.0)
    kept = jnp.sum(kept.reshape(samples, rows, shape[1]), axis=1)
    bank_of = lax.div(lax.broadcasted_iota(jnp.int32, kept.shape, 1), rows)
    lane = lax.broadcasted_iota(jnp.int32, (samples, 128), 1)
    table = jnp.zeros((samples, 128), F32)
    for k in range(banks):
        total = jnp.sum(jnp.where(bank_of == k, kept, 0.0), axis=1, keepdims=True)
        table = jnp.where(lane == lane0 + k, total, table)
    for d in range(samples):
        b = jnp.bitwise_xor(me, d)
        line = jnp.broadcast_to(table[d : d + 1], dcoef.shape[1:])
        dcoef[b] = line + more[b] if has_more else line
    for k in range(banks):
        weights = [coefs[jnp.bitwise_xor(me, d), k] for d in range(samples)]

        def step(t, carry, k=k, weights=weights):
            lanes = pl.ds(pl.multiple_of(t * width, width), width)
            total = weights[0] * all_grads[0:rows, lanes].astype(F32)
            for d in range(1, samples):
                total = total + weights[d] * all_grads[d * rows : (d + 1) * rows, lanes].astype(F32)
            update[k, t] = total
            return carry

        lax.fori_loop(0, taps, step, 0)


def logit_body(got, fine_coefs, coarse_coefs, fine_out, coarse_out):
    me, _, _, _ = place()
    banks = fine_coefs.shape[1]
    total = jnp.sum(got[...], axis=0, keepdims=True)
    for lane0, coefs, out in ((0, fine_coefs, fine_out), (banks, coarse_coefs, coarse_out)):
        own = coefs[pl.ds(me, 1), :]
        mine = total[:, lane0 : lane0 + banks]
        out[...] = own * (mine - jnp.sum(own * mine, axis=1, keepdims=True))


def shape(*dims, dtype=BF16):
    return jax.ShapeDtypeStruct(dims, dtype)


def pair_device(fi, fu, fb, fc, ci, cu, cb, cc):
    pairs = lax.axis_size("chan")
    count = lax.axis_size("batch")
    fine_side, coarse_side = fi.shape[1], ci.shape[1]
    fine_px, coarse_px = fine_side**2, coarse_side**2
    channels = fi.shape[3]
    banks, taps, rows, width = fb.shape
    block = 2 * rows
    span = taps * width
    fx, fup = fi.reshape(fine_px, channels), fu.reshape(fine_px, width)
    cx, cup = ci.reshape(coarse_px, channels), cu.reshape(coarse_px, width)

    def over_batch(x, d):
        return lax.ppermute(x, "batch", [(i, i ^ d) for i in range(count)])

    def over_chan(x, d):
        return lax.ppermute(x, "chan", [(i, i ^ d) for i in range(pairs)])

    other_fb = over_batch(fb, 1)
    other_cb = over_batch(cb, 1)

    packed = call(
        functools.partial(pack_body, pairs),
        [shape(2 * coarse_px, block)] * pairs, 0, 2,
        nbytes=10 * coarse_px * block * pairs, name="pack",
    )(cx, cup)
    bufs = [packed[0]] + [over_batch(packed[d], 2 * d) for d in range(1, pairs)]

    mixed = call(
        functools.partial(mix_body, pairs),
        [shape(block, span)] * pairs, 1, 2,
        flops=2 * banks * pairs * block * span, nbytes=6 * banks * rows * span, name="mix",
    )(fc, fb, other_fb)
    mixed = [mixed[0]] + [over_batch(mixed[d], 2 * d) for d in range(1, pairs)]

    fine_grads = call(
        functools.partial(grads_body, pairs, fine_side),
        [shape(block, span)] * pairs, 0, 2,
        [pltpu.VMEM((fine_px, span), BF16), pltpu.VMEM((channels, span), BF16)],
        flops=2 * fine_px * channels * span, nbytes=4 * fine_px * channels, name="grads",
    )(fx, fup)

    coarse = call(
        functools.partial(coarse_body, pairs, coarse_side),
        [shape(coarse_px, block)] * pairs + [shape(block, span)] * pairs, 1, 2 + pairs,
        [pltpu.VMEM((coarse_px, span), BF16), pltpu.VMEM((pairs, coarse_px, block), BF16)]
        + [pltpu.VMEM((block, span), BF16)] * pairs,
        flops=4 * pairs * coarse_px * block * span, nbytes=8 * banks * rows * span, name="coarse",
    )(cc, cb, other_cb, *bufs)
    parts, coarse_grads = coarse[:pairs], coarse[pairs:]

    def homeward(x, e):
        moves = []
        for b in range(count):
            for c in range(pairs):
                moves.append((b * pairs + c, (2 * (c ^ e) + b % 2) * pairs + b // 2))
        return lax.ppermute(x, ("batch", "chan"), moves)

    parts = [homeward(parts[e], e) for e in range(pairs)]
    coarse_other = [over_batch(g, 1) for g in coarse_grads]

    fine_own = [fine_grads[0]] + [over_batch(fine_grads[d], 2 * d) for d in range(1, pairs)]
    fine_other = [over_batch(g, 1) for g in fine_own]

    def update(coefs, bank, own, other, lane0, more):
        return call(
            functools.partial(update_body, pairs, lane0, more is not None),
            [shape(banks, taps, rows, width, dtype=F32), shape(count, pairs, 128, dtype=F32)],
            1, 1 + 2 * pairs + (more is not None),
            [pltpu.VMEM((count * rows, span), BF16), pltpu.VMEM((banks * rows, span), BF16)],
            flops=4 * banks * count * rows * span, nbytes=8 * banks * rows * span, name="update",
        )(coefs, bank, *own, *other, *(() if more is None else (more,)))

    coarse_update, coarse_dcoef = update(cc, cb, coarse_grads, coarse_other, banks, None)

    fine_parts = call(
        functools.partial(delta_body, pairs, fine_side),
        [shape(fine_px, block)] * pairs, 0, 1 + pairs,
        [pltpu.VMEM((fine_px, span), BF16), pltpu.VMEM((channels, span), BF16)],
        flops=2 * fine_px * channels * span, nbytes=4 * fine_px * channels, name="delta",
    )(fup, *mixed)
    fine_parts = [fine_parts[0]] + [over_chan(fine_parts[s], s) for s in range(1, pairs)]

    fine_update, dcoef = update(fc, fb, fine_own, fine_other, 0, coarse_dcoef)
    dcoef = dcoef.reshape(count * pairs, 128)
    got = lax.all_to_all(dcoef, ("batch", "chan"), 0, 0, tiled=True)
    fine_logit, coarse_logit = call(
        logit_body, [shape(1, banks, dtype=F32)] * 2, 0, 3, name="logit",
    )(got, fc, cc)

    def total(pieces):
        out = pieces[0].astype(F32)
        for piece in pieces[1:]:
            out = out + piece.astype(F32)
        return out.astype(BF16)

    fine_delta = total(fine_parts).reshape(1, fine_side, fine_side, block)
    coarse_delta = total(parts).reshape(1, coarse_side, coarse_side, block)
    return (fine_delta, fine_update, fine_logit, coarse_delta, coarse_update, coarse_logit)


def fits_pairs(mesh, fi, fu, fb, fc, ci, cu, cb, cc):
    count, pairs = mesh.shape["batch"], mesh.shape["chan"]
    rows, width, block = fb.shape[2] // count, fb.shape[3] // pairs, fb.shape[2] // pairs
    banks = fb.shape[0]
    return (
        count == 2 * pairs
        and pairs & (pairs - 1) == 0
        and fi.shape[0] == count
        and fb.shape == cb.shape
        and fi.shape[3] == fb.shape[2]
        and rows % 16 == 0
        and width % 128 == 0
        and block == width
        and 2 * banks <= 128
        and all(x.shape[1] == x.shape[2] and x.shape[1] % 16 == 0 for x in (fi, ci))
    )


def solution(mesh):
    def step(*args):
        body = pair_device if fits_pairs(mesh, *args) else plain_device
        return jax.shard_map(
            body,
            mesh=mesh,
            in_specs=(
                P("batch", None, None, None),
                P("batch", None, None, "chan"),
                P(None, None, "batch", "chan"),
                P(),
                P("batch", None, None, None),
                P("batch", None, None, "chan"),
                P(None, None, "batch", "chan"),
                P(),
            ),
            out_specs=(
                P("batch", None, None, "chan"),
                P(None, None, "batch", "chan"),
                P("batch", None),
                P("batch", None, None, "chan"),
                P(None, None, "batch", "chan"),
                P("batch", None),
            ),
            check_vma=False,
        )(*args)

    return step
```

```python
import functools

import jax
import jax.numpy as jnp
from jax import lax
from jax.experimental import pallas as pl
from jax.experimental.pallas import tpu as pltpu
from jax.sharding import PartitionSpec as P


HIGH = lax.Precision.HIGHEST
F32 = jnp.float32
BF16 = jnp.bfloat16


def shifted(padded, row_shift, col_shift, side):
    window = padded[:, row_shift : row_shift + side, col_shift : col_shift + side, :]
    return window.reshape(window.shape[0], side * side, window.shape[3])


def local_grads(inputs, upstream, kernels, side):
    samples_here = inputs.shape[0]
    pad_in = jnp.pad(inputs, ((0, 0), (1, 1), (1, 1), (0, 0)))
    pad_up = jnp.pad(upstream, ((0, 0), (1, 1), (1, 1), (0, 0)))
    flat_up = upstream.reshape(samples_here, side * side, upstream.shape[3])
    delta = jnp.zeros((samples_here, side * side, inputs.shape[3]), F32)
    grad_taps = []
    for row_shift in range(3):
        for col_shift in range(3):
            tap = 3 * row_shift + col_shift
            window_in = shifted(pad_in, row_shift, col_shift, side)
            window_up = shifted(pad_up, 2 - row_shift, 2 - col_shift, side)
            grad_taps.append(
                jnp.einsum("bpc,bpo->bco", window_in, flat_up, preferred_element_type=F32) / side
            )
            delta = delta + jnp.einsum(
                "bpo,bco->bpc", window_up, kernels[:, tap], preferred_element_type=F32
            )
    return (delta.reshape(samples_here, side, side, inputs.shape[3]), jnp.stack(grad_taps, axis=1))


def plain_layer(inputs, upstream, bank_part, coefs):
    side = inputs.shape[1]
    flat_bank = bank_part.reshape(bank_part.shape[0], -1).astype(F32)
    mixed_all = jnp.dot(coefs, flat_bank, precision=HIGH)
    mixed_all = mixed_all.reshape((coefs.shape[0],) + bank_part.shape[1:]).astype(BF16)
    kernels = lax.all_to_all(mixed_all, "batch", split_axis=0, concat_axis=2, tiled=True)
    delta, kernel_grad = local_grads(inputs, upstream, kernels, side)
    delta_total = lax.psum(delta.astype(BF16), "chan").astype(F32)
    width = delta.shape[3] // lax.axis_size("chan")
    delta_part = lax.dynamic_slice_in_dim(delta_total, lax.axis_index("chan") * width, width, 3)
    moved = lax.all_to_all(
        kernel_grad.astype(BF16), "batch", split_axis=2, concat_axis=0, tiled=True
    ).astype(kernel_grad.dtype)
    flat_grads = moved.reshape(moved.shape[0], -1)
    update = jnp.dot(coefs.T, flat_grads, precision=HIGH).reshape(bank_part.shape)
    dcoef_part = lax.dot_general(flat_grads, flat_bank, (((1,), (1,)), ((), ())), precision=HIGH)
    return (delta_part.astype(BF16), update, dcoef_part)


def plain_logits(coefs, totals, samples_here):
    first_row = lax.axis_index("batch") * samples_here
    own_coefs = lax.dynamic_slice_in_dim(coefs, first_row, samples_here, 0)
    own_totals = lax.dynamic_slice_in_dim(totals, first_row, samples_here, 0)
    return own_coefs * (own_totals - jnp.sum(own_coefs * own_totals, axis=1, keepdims=True))


def plain_device(fi, fu, fb, fc, ci, cu, cb, cc):
    fine_delta, fine_update, fine_partial = plain_layer(fi, fu, fb, fc)
    coarse_delta, coarse_update, coarse_partial = plain_layer(ci, cu, cb, cc)
    fine_total, coarse_total = lax.psum((fine_partial, coarse_partial), ("batch", "chan"))
    fine_logit = plain_logits(fc, fine_total, fi.shape[0])
    coarse_logit = plain_logits(cc, coarse_total, fi.shape[0])
    return (fine_delta, fine_update, fine_logit, coarse_delta, coarse_update, coarse_logit)


def place():
    me = lax.axis_index("batch")
    return me, lax.div(me, 2), lax.rem(me, 2), lax.axis_index("chan")


def smem(n):
    return [pl.BlockSpec(memory_space=pltpu.SMEM) for _ in range(n)]


def hbm(n):
    return [pl.BlockSpec(memory_space=pl.ANY) for _ in range(n)]


def vmem(n):
    return [pl.BlockSpec(memory_space=pltpu.VMEM) for _ in range(n)]


def call(body, out_shapes, in_specs, out_specs, scratch=(), flops=0, nbytes=0, alone=False, grant=16 * 1024 * 1024):
    return pl.pallas_call(
        body,
        out_shape=out_shapes,
        in_specs=in_specs,
        out_specs=out_specs,
        scratch_shapes=list(scratch),
        compiler_params=pltpu.CompilerParams(vmem_limit_bytes=None if alone else grant),
        cost_estimate=pl.CostEstimate(flops=flops, bytes_accessed=nbytes, transcendentals=0),
    )


def start(src, dst, sem):
    copy = pltpu.make_async_copy(src, dst, sem)
    copy.start()
    return copy


def fill_windows(up, side, ref):
    pixels, width = up.shape
    wide = up.astype(F32)
    col = lax.rem(lax.broadcasted_iota(jnp.int32, (pixels, width), 0), side)
    zeros = jnp.zeros((side, 3 * width), BF16)
    ref[0:side, :] = zeros
    ref[side + pixels :, :] = zeros
    body = slice(side, side + pixels)
    ref[body, 0:width] = jnp.where(col == side - 1, 0.0, pltpu.roll(wide, pixels - 1, 0)).astype(BF16)
    ref[body, width : 2 * width] = up
    ref[body, 2 * width :] = jnp.where(col == 0, 0.0, pltpu.roll(wide, 1, 0)).astype(BF16)


def window(ref, side, dy):
    first = (2 - dy) * side
    return ref[first : first + ref.shape[0] - 2 * side, :]


def all_windows(ref, side):
    return jnp.concatenate([window(ref, side, dy) for dy in range(3)], axis=1)


def dot_nt(a, b):
    return lax.dot_general(a, b, (((1,), (1,)), ((), ())), preferred_element_type=F32)


def dot_tn(a, b):
    return lax.dot_general(a, b, (((0,), (0,)), ((), ())), preferred_element_type=F32)


def front_body(pairs, side, fx, fup, *rest):
    outs, (v_fx, v_fup, windows, staged, sem_in, sem_out) = rest[:pairs], rest[pairs:]
    _, pair, _, _ = place()
    loads = [start(fup, v_fup, sem_in.at[0]), start(fx, v_fx, sem_in.at[1])]
    loads[0].wait()
    fill_windows(v_fup[...], side, windows)
    loads[1].wait()
    got = dot_tn(v_fx[...], all_windows(windows, side))
    staged[...] = (got * (1.0 / side)).astype(BF16)
    rows = staged.shape[0] // pairs
    stores = []
    for d, out in enumerate(outs):
        first = pl.multiple_of(jnp.bitwise_xor(pair, d) * rows, rows)
        stores.append(start(staged.at[pl.ds(first, rows), :], out, sem_out.at[d]))
    for store in stores:
        store.wait()


def load_banks(own, other, v_banks, sems):
    taps, width = own.shape[1], own.shape[3]
    loads = []
    for t in range(taps):
        lanes = slice(t * width, (t + 1) * width)
        loads.append(
            [
                start(bank.at[:, t], v_banks.at[src, :, :, lanes], sems.at[src, t])
                for src, bank in enumerate((own, other))
            ]
        )
    return loads


def half_row(src, rows):
    _, _, half, _ = place()
    return pl.multiple_of((half if src == 0 else 1 - half) * rows, rows)


def spread(weights, chunk):
    count, terms = len(weights), len(weights[0])
    dims = (chunk, terms * chunk)
    lane = lax.broadcasted_iota(jnp.int32, dims, 1)
    same = lax.broadcasted_iota(jnp.int32, dims, 0) == lax.rem(lane, chunk)
    term = lax.div(lane[0:8], chunk)
    high, low = [], []
    for n in range(count):
        line = jnp.full((8, terms * chunk), weights[n][0], F32)
        for k in range(1, terms):
            line = jnp.where(term == k, weights[n][k], line)
        value = jnp.where(same, jnp.concatenate([line] * (chunk // 8), axis=0), 0.0)
        rounded = value.astype(BF16)
        high.append(rounded)
        low.append((value - rounded.astype(F32)).astype(BF16))
    return jnp.concatenate(high + low, axis=0)


def dot_nn(a, b):
    return lax.dot_general(a, b, (((1,), (0,)), ((), ())), preferred_element_type=F32)


def chunk_of(rows, terms):
    return max(16, min(rows, 256 // terms))


def mix_weights(pairs, coefs):
    me, _, _, _ = place()
    banks = coefs.shape[1]
    return [[coefs[jnp.bitwise_xor(me, 2 * d), k] for k in range(banks)] for d in range(pairs)]


def pack_body(pairs, cx, cup, *rest):
    packs, (v_x, v_up, sem_in, sem_out) = rest[:pairs], rest[pairs:]
    _, pair, _, _ = place()
    pixels, width = v_up.shape
    loads = [start(cup, v_up, sem_in.at[0]), start(cx, v_x, sem_in.at[1])]
    loads[0].wait()
    stores = [start(v_up, out.at[0:pixels, :], sem_out.at[0, d]) for d, out in enumerate(packs)]
    loads[1].wait()
    for d, out in enumerate(packs):
        first = pl.multiple_of(jnp.bitwise_xor(pair, d) * width, width)
        stores.append(start(v_x.at[:, pl.ds(first, width)], out.at[pixels:, :], sem_out.at[1, d]))
    for store in stores:
        store.wait()


def tables_body(pairs, chunk, fine_coefs, coarse_coefs, *tables):
    me, _, _, _ = place()
    samples = 2 * pairs
    for n, coefs in enumerate((fine_coefs, coarse_coefs)):
        banks = coefs.shape[1]
        to_updates, row = tables[2 * n : 2 * n + 2]
        weights = [[coefs[jnp.bitwise_xor(me, d), k] for d in range(samples)] for k in range(banks)]
        to_updates[...] = spread(weights, chunk)
        lane = lax.broadcasted_iota(jnp.int32, row.shape, 1)
        line = jnp.zeros(row.shape, F32)
        for k in range(banks):
            line = jnp.where(lane == k, coefs[me, k], line)
        row[...] = line


def mix_lanes(pairs, table, v_banks, staged, lanes):
    _, banks, rows, _ = v_banks.shape
    chunk = table.shape[1] // banks
    for src in range(2):
        base = half_row(src, rows)
        for at in range(0, rows, chunk):
            right = v_banks[src, :, at : at + chunk, lanes]
            got = dot_nn(table, right.reshape(banks * chunk, right.shape[2]))
            got = (got[: pairs * chunk] + got[pairs * chunk :]).astype(BF16)
            into = pl.ds(pl.multiple_of(base + at, 16), chunk)
            for d in range(pairs):
                staged[d, into, lanes] = got[d * chunk : (d + 1) * chunk]


def mix_body(pairs, coefs, own, other, *rest):
    outs, (s_coefs, v_banks, staged, sem_coefs, sem_in, sem_out) = rest[:pairs], rest[pairs:]
    taps, width = own.shape[1], own.shape[3]
    first = start(coefs, s_coefs, sem_coefs)
    loads = load_banks(own, other, v_banks, sem_in)
    first.wait()
    table = spread(mix_weights(pairs, s_coefs), chunk_of(own.shape[2], own.shape[0]))
    stores = []
    for t in range(0, taps, 3):
        for some in loads[t : t + 3]:
            for load in some:
                load.wait()
        lanes = slice(t * width, (t + 3) * width)
        mix_lanes(pairs, table, v_banks, staged, lanes)
        for d, out in enumerate(outs):
            stores.append(start(staged.at[d, :, lanes], out.at[:, lanes], sem_out.at[d, t]))
    for store in stores:
        store.wait()


def delta_body(pairs, side, up, *rest):
    mixed, outs = rest[:pairs], rest[pairs : 2 * pairs]
    v_up, windows, kernels, staged, sem_in, sem_out = rest[2 * pairs :]
    _, pair, _, chan = place()
    rows = kernels.shape[0] // pairs
    first_load = start(up, v_up, sem_in.at[pairs])
    loads = []
    for d in range(pairs):
        slot = jnp.bitwise_xor(jnp.bitwise_xor(pair, d), chan)
        at = pl.multiple_of(slot * rows, rows)
        loads.append(start(mixed[d], kernels.at[pl.ds(at, rows), :], sem_in.at[d]))
    first_load.wait()
    fill_windows(v_up[...], side, windows)
    for load in loads:
        load.wait()
    stores = []
    got = dot_nt(all_windows(windows, side), kernels[...])
    for slot in range(pairs):
        staged[slot] = got[:, slot * rows : (slot + 1) * rows].astype(BF16)
        stores.append(start(staged.at[slot], outs[slot], sem_out.at[slot]))
    for store in stores:
        store.wait()


def dcoef_rows(pairs, grads, v_banks, lane0):
    _, banks, rows, span = v_banks.shape
    chunk = chunk_of(rows, banks)
    cross = None
    for src in range(2):
        for at in range(0, rows, chunk):
            first = pl.multiple_of(half_row(src, rows) + at, 16)
            left = grads[:, pl.ds(first, chunk), :].reshape(pairs * chunk, span)
            right = v_banks[src, :, at : at + chunk, :].reshape(banks * chunk, span)
            one = dot_nt(left, right)
            cross = one if cross is None else cross + one
    row = lax.rem(lax.broadcasted_iota(jnp.int32, cross.shape, 0), chunk)
    col = lax.rem(lax.broadcasted_iota(jnp.int32, cross.shape, 1), chunk)
    kept = jnp.where(row == col, cross, 0.0)
    kept = jnp.sum(kept.reshape(pairs, chunk, banks * chunk), axis=1)
    bank_of = lax.div(lax.broadcasted_iota(jnp.int32, kept.shape, 1), chunk)
    lane = lax.broadcasted_iota(jnp.int32, (pairs, 128), 1)
    total = jnp.zeros((pairs, 128), F32)
    for k in range(banks):
        one = jnp.sum(jnp.where(bank_of == k, kept, 0.0), axis=1, keepdims=True)
        total = jnp.where(lane == lane0 + k, one, total)
    return total


def coarse_body(pairs, side, coefs, own, other, *rest):
    ups, parts, rest = rest[:pairs], rest[pairs : 2 * pairs], rest[2 * pairs :]
    s_coefs, v_banks, v_mixed, v_ups, windows, v_parts, sem_coefs, sem_bank, sem_in, sem_out = rest
    taps, width = own.shape[1], own.shape[3]
    pixels = side * side
    first = start(coefs, s_coefs, sem_coefs)
    loads = [start(ups[d].at[0:pixels, :], v_ups.at[d], sem_in.at[d]) for d in range(pairs)]
    bank_loads = load_banks(own, other, v_banks, sem_bank)
    first.wait()
    table = spread(mix_weights(pairs, s_coefs), chunk_of(own.shape[2], own.shape[0]))
    for t in range(0, taps, 3):
        for some in bank_loads[t : t + 3]:
            for load in some:
                load.wait()
        mix_lanes(pairs, table, v_banks, v_mixed, slice(t * width, (t + 3) * width))
    stores = []
    third = windows.shape[1]
    for d in range(pairs):
        loads[d].wait()
        fill_windows(v_ups[d], side, windows)
        part = None
        for dy in range(3):
            one = dot_nt(window(windows, side, dy), v_mixed[d, :, dy * third : (dy + 1) * third])
            part = one if part is None else part + one
        v_parts[d] = part.astype(BF16)
        stores.append(start(v_parts.at[d], parts[d], sem_out.at[d]))
    for store in stores:
        store.wait()


def calm_body(pairs, side, own, other, *rest):
    bufs, grads, table, rest = rest[:pairs], rest[pairs : 2 * pairs], rest[2 * pairs], rest[2 * pairs + 1 :]
    v_banks, v_bufs, windows, v_grads, sem_bank, sem_in, sem_out = rest
    pixels = side * side
    loads = [start(bufs[d], v_bufs.at[d], sem_in.at[d]) for d in range(pairs)]
    bank_loads = load_banks(own, other, v_banks, sem_bank)
    stores = []
    for d in range(pairs):
        loads[d].wait()
        fill_windows(v_bufs[d, 0:pixels, :], side, windows)
        got = dot_tn(v_bufs[d, pixels:, :], all_windows(windows, side))
        v_grads[d] = (got * (1.0 / side)).astype(BF16)
        stores.append(start(v_grads.at[d], grads[d], sem_out.at[d]))
    for some in bank_loads:
        for load in some:
            load.wait()
    table[...] = dcoef_rows(pairs, v_grads, v_banks, own.shape[0])
    for store in stores:
        store.wait()


def as_pair(rows):
    high = rows.astype(BF16)
    return jnp.concatenate([high, (rows - high.astype(F32)).astype(BF16)], axis=0)


def from_pair(both):
    wide = both.astype(F32)
    return wide[0:8] + wide[8:16]


def late_body(pairs, own, other, more, *rest):
    gots, parts, outs = rest[:pairs], rest[pairs : 2 * pairs - 1], rest[2 * pairs - 1 : 3 * pairs - 2]
    mine, v_banks, v_gots, v_out, sem_bank, sem_in, sem_part, sem_out = rest[3 * pairs - 2 :]
    loads = [[start(gots[d], v_gots.at[d], sem_in.at[d]) for d in range(pairs)]]
    loads += load_banks(own, other, v_banks, sem_bank)
    pixels = parts[0].shape[0]
    loads.append(
        [start(parts[d], v_out.at[d, 0:pixels, :], sem_part.at[d]) for d in range(pairs - 1)]
    )
    for some in loads:
        for load in some:
            load.wait()
    total = dcoef_rows(pairs, v_gots, v_banks, 0) + more[...]
    mine[...] = jnp.broadcast_to(total[0:1], mine.shape)
    stores = []
    for d in range(pairs - 1):
        v_out[d, pixels:, :] = as_pair(jnp.broadcast_to(total[d + 1 : d + 2], mine.shape))
        stores.append(start(v_out.at[d], outs[d], sem_out.at[d]))
    for store in stores:
        store.wait()


def slot_body(pairs, first_part, first_row, *rest):
    gots, slots, rest = rest[: pairs - 1], rest[pairs - 1 : 2 * pairs - 1], rest[2 * pairs - 1 :]
    mine, v_slots, sem_in, sem_out = rest
    _, pair, _, chan = place()
    pixels = first_part.shape[0]
    loads, at = [], []
    for d in range(pairs):
        slot = jnp.bitwise_xor(jnp.bitwise_xor(pair, d), chan)
        at.append(slot)
        if d == 0:
            loads.append(start(first_part, v_slots.at[slot, 0:pixels, :], sem_in.at[0]))
        else:
            loads.append(start(gots[d - 1], v_slots.at[slot], sem_in.at[d]))
    for load in loads:
        load.wait()
    total = first_row[...]
    for d in range(1, pairs):
        total = total + from_pair(v_slots[at[d], pixels:, :])
    both = as_pair(total)
    mine[...] = from_pair(both)
    for s in range(pairs):
        v_slots[s, pixels:, :] = both
    stores = [start(v_slots.at[s], slots[s], sem_out.at[s]) for s in range(pairs)]
    for store in stores:
        store.wait()


def update_body(pairs, layers, *rest):
    samples = 2 * pairs
    tables, rest = rest[:layers], rest[layers:]
    all_gots, rest = rest[: layers * samples], rest[layers * samples :]
    updates, (v_grads, staged, sem_in, sem_out) = rest[:layers], rest[layers:]
    _, _, half, _ = place()
    banks, taps, rows, width = updates[0].shape
    first = pl.multiple_of(half * rows, rows)
    loads = []
    for n in range(layers):
        gots = all_gots[n * samples : (n + 1) * samples]
        for d in range(samples):
            src = gots[d % 2 * pairs + d // 2].at[pl.ds(first, rows), 0 : taps * width]
            loads.append(start(src, v_grads.at[n, d], sem_in.at[n, d]))
    for load in loads:
        load.wait()
    chunk = chunk_of(rows, samples)
    stores = []
    for n in range(layers):
        table = tables[n][...]
        half_table = banks * chunk
        for at in range(0, rows, chunk):
            right = v_grads[n, :, at : at + chunk, :].reshape(samples * chunk, taps * width)
            got = dot_nn(table, right)
            got = got[:half_table] + got[half_table:]
            for k in range(banks):
                for t in range(taps):
                    staged[n, k, t, at : at + chunk, :] = got[
                        k * chunk : (k + 1) * chunk, t * width : (t + 1) * width
                    ]
            some = slice(at, at + chunk)
            stores.append(
                start(staged.at[n, :, :, some], updates[n].at[:, :, some], sem_out.at[n, at // chunk])
            )
    for store in stores:
        store.wait()


def final_body(pairs, banks, mine, fine_row, coarse_row, *rest):
    pieces, rest = rest[: 2 * pairs], rest[2 * pairs :]
    fine_out, coarse_out, fine_delta, coarse_delta, v_fine, v_coarse, sem_in, sem_out = rest
    layers = ((v_fine, fine_delta), (v_coarse, coarse_delta))
    loads = [
        [
            start(pieces[n * pairs + d], v.at[d], sem_in.at[n, d])
            for d in range(pairs)
        ]
        for n, (v, _) in enumerate(layers)
    ]
    stores = []
    for n, (v, out) in enumerate(layers):
        for load in loads[n]:
            load.wait()
        pixels = out.shape[0]
        total = v[0, 0:pixels, :].astype(F32)
        for d in range(1, pairs):
            total = total + v[d, 0:pixels, :].astype(F32)
        v[pairs, 0:pixels, :] = total.astype(BF16)
        stores.append(start(v.at[pairs, 0:pixels, :], out, sem_out.at[n]))
    total = mine[...]
    for d in range(1, pairs):
        total = total + from_pair(v_coarse[d, pixels:, :])
    for lane0, row, out in ((0, fine_row, fine_out), (banks, coarse_row, coarse_out)):
        own = row[:, 0:banks]
        some = total[0:1, lane0 : lane0 + banks]
        out[...] = own * (some - jnp.sum(own * some, axis=1, keepdims=True))
    for store in stores:
        store.wait()


def shape(*dims, dtype=BF16):
    return jax.ShapeDtypeStruct(dims, dtype)


def pair_device(fi, fu, fb, fc, ci, cu, cb, cc):
    return pair_steps(fi, fu, fb, fc, ci, cu, cb, cc)


def pair_steps(fi, fu, fb, fc, ci, cu, cb, cc):
    pairs = lax.axis_size("chan")
    count = lax.axis_size("batch")
    fine_side, coarse_side = fi.shape[1], ci.shape[1]
    fine_px, coarse_px = fine_side**2, coarse_side**2
    channels = fi.shape[3]
    banks, taps, rows, width = fb.shape
    block = 2 * rows
    span = taps * width
    fx, fup = fi.reshape(fine_px, channels), fu.reshape(fine_px, width)
    cx, cup = ci.reshape(coarse_px, channels), cu.reshape(coarse_px, width)

    def over_batch(x, d):
        return lax.ppermute(x, "batch", [(i, i ^ d) for i in range(count)])

    def over_chan(x, d):
        return lax.ppermute(x, "chan", [(i, i ^ d) for i in range(pairs)])

    def send(move, pieces, distances):
        out = []
        for piece, d in zip(pieces, distances):
            out.append(move(piece, d))
        return out

    def to_pairs(pieces):
        moved = send(lambda x, d: over_batch(x, 2 * d), pieces[1:], range(1, pairs))
        return [pieces[0]] + moved

    dma = pltpu.SemaphoreType.DMA
    work = 2 * fine_px * channels * span
    bank_bytes = 2 * banks * rows * span

    other_fb, other_cb = send(lambda x, d: over_batch(x, 1), (fb, cb), range(2))

    def mix_scratch():
        return [pltpu.SMEM(fc.shape, F32), pltpu.VMEM((2, banks, rows, span), BF16), pltpu.VMEM((pairs, block, span), BF16)]

    packs = call(
        functools.partial(pack_body, pairs),
        [shape(2 * coarse_px, block)] * pairs, hbm(2), hbm(pairs),
        [
            pltpu.VMEM((coarse_px, channels), BF16), pltpu.VMEM((coarse_px, width), BF16),
            dma((2,)), dma((2, pairs)),
        ],
        nbytes=bank_bytes, alone=True,
    )(cx, cup)
    bufs = to_pairs(packs)
    chunk = chunk_of(rows, count)
    fine_sum, fine_row, coarse_sum, coarse_row = call(
        functools.partial(tables_body, pairs, chunk),
        [shape(2 * banks * chunk, count * chunk), shape(1, 128, dtype=F32)] * 2,
        smem(2), vmem(4), flops=work, nbytes=bank_bytes,
    )(fc, cc)

    mixed = call(
        functools.partial(mix_body, pairs),
        [shape(block, span)] * pairs, hbm(3), hbm(pairs),
        mix_scratch() + [dma, dma((2, taps)), dma((pairs, taps))],
        flops=4 * banks * pairs * block * span, nbytes=3 * bank_bytes,
    )(fc, fb, other_fb)
    mixed = to_pairs(mixed)

    parts = call(
        functools.partial(coarse_body, pairs, coarse_side),
        [shape(coarse_px, block)] * pairs, hbm(3 + pairs), hbm(pairs),
        mix_scratch() + [
            pltpu.VMEM((pairs, coarse_px, width), BF16),
            pltpu.VMEM((coarse_px + 2 * coarse_side, 3 * width), BF16),
            pltpu.VMEM((pairs, coarse_px, block), BF16),
            dma, dma((2, taps)), dma((pairs,)), dma((pairs,)),
        ],
        flops=work, nbytes=3 * bank_bytes,
    )(cc, cb, other_cb, *bufs)

    front = call(
        functools.partial(front_body, pairs, fine_side),
        [shape(block, span)] * pairs, hbm(2), hbm(pairs),
        [
            pltpu.VMEM((fine_px, channels), BF16), pltpu.VMEM((fine_px, width), BF16),
            pltpu.VMEM((fine_px + 2 * fine_side, 3 * width), BF16), pltpu.VMEM((channels, span), BF16),
            dma((2,)), dma((pairs,)),
        ],
        flops=work, nbytes=5 * fine_px * channels,
    )(fx, fup)
    fine_own = to_pairs(front)

    fine_parts = call(
        functools.partial(delta_body, pairs, fine_side),
        [shape(fine_px, block)] * pairs, hbm(1 + pairs), hbm(pairs),
        [
            pltpu.VMEM((fine_px, width), BF16),
            pltpu.VMEM((fine_px + 2 * fine_side, 3 * width), BF16),
            pltpu.VMEM((channels, span), BF16), pltpu.VMEM((pairs, fine_px, block), BF16),
            dma((pairs + 1,)), dma((pairs,)),
        ],
        flops=work, nbytes=5 * fine_px * channels,
    )(fup, *mixed)
    fine_parts = [fine_parts[0]] + send(over_chan, fine_parts[1:], range(1, pairs))

    tile = shape(8, 128, dtype=F32)
    loaded = [shape(coarse_px + 16, block)]
    calm = call(
        functools.partial(calm_body, pairs, coarse_side),
        [shape(block, span)] * pairs + [shape(pairs, 128, dtype=F32)],
        hbm(2 + pairs), hbm(pairs) + vmem(1),
        [
            pltpu.VMEM((2, banks, rows, span), BF16), pltpu.VMEM((pairs, 2 * coarse_px, block), BF16),
            pltpu.VMEM((coarse_px + 2 * coarse_side, 3 * width), BF16),
            pltpu.VMEM((pairs, block, span), BF16),
            dma((2, taps)), dma((pairs,)), dma((pairs,)),
        ],
        flops=work, nbytes=3 * bank_bytes,
    )(cb, other_cb, *bufs)
    coarse_own, coarse_dcoef = calm[:pairs], calm[pairs]

    late = call(
        functools.partial(late_body, pairs),
        loaded * (pairs - 1) + [tile],
        hbm(2) + vmem(1) + hbm(2 * pairs - 1), hbm(pairs - 1) + vmem(1),
        [
            pltpu.VMEM((2, banks, rows, span), BF16), pltpu.VMEM((pairs, block, span), BF16),
            pltpu.VMEM((pairs - 1, coarse_px + 16, block), BF16),
            dma((2, taps)), dma((pairs,)), dma((pairs - 1,)), dma((pairs - 1,)),
        ],
        flops=work, nbytes=3 * bank_bytes,
    )(fb, other_fb, coarse_dcoef, *fine_own, *parts[1:])
    tiles = send(lambda x, d: over_batch(x, 2 * d), late[: pairs - 1], range(1, pairs))

    slots = call(
        functools.partial(slot_body, pairs),
        loaded * pairs + [tile],
        hbm(1) + vmem(1) + hbm(pairs - 1), hbm(pairs) + vmem(1),
        [pltpu.VMEM((pairs, coarse_px + 16, block), BF16), dma((pairs,)), dma((pairs,))],
        nbytes=4 * pairs * coarse_px * block,
    )(parts[0], late[pairs - 1], *tiles)
    slots, mine = slots[:pairs], slots[pairs]
    slots = [slots[0]] + send(over_chan, slots[1:], range(1, pairs))

    swapped = [
        send(lambda x, d: over_batch(x, 1), own, range(pairs))
        for own in (fine_own, coarse_own)
    ]

    def update(table, own, others):
        return call(
            functools.partial(update_body, pairs, 1),
            [shape(banks, taps, rows, width, dtype=F32)], vmem(1) + hbm(2 * pairs), hbm(1),
            [
                pltpu.VMEM((1, count, rows, span), BF16),
                pltpu.VMEM((1, banks, taps, rows, width), F32),
                dma((1, count)), dma((1, taps)),
            ],
            flops=2 * banks * count * rows * span, nbytes=3 * bank_bytes,
        )(table, *own, *others)[0]

    fine_update = update(fine_sum, fine_own, swapped[0])
    coarse_update = update(coarse_sum, coarse_own, swapped[1])

    fine_logit, coarse_logit, fine_delta, coarse_delta = call(
        functools.partial(final_body, pairs, banks),
        [shape(1, banks, dtype=F32)] * 2 + [shape(fine_px, block), shape(coarse_px, block)],
        vmem(3) + hbm(2 * pairs), vmem(2) + hbm(2),
        [
            pltpu.VMEM((pairs + 1, fine_px, block), BF16),
            pltpu.VMEM((pairs + 1, coarse_px + 16, block), BF16), dma((2, pairs)), dma((2,)),
        ],
        nbytes=2 * fine_px * channels,
    )(mine, fine_row, coarse_row, *fine_parts, *slots)
    fine_delta = fine_delta.reshape(1, fine_side, fine_side, block)
    coarse_delta = coarse_delta.reshape(1, coarse_side, coarse_side, block)
    return (fine_delta, fine_update, fine_logit, coarse_delta, coarse_update, coarse_logit)


def fits_pairs(mesh, fi, fu, fb, fc, ci, cu, cb, cc):
    count, pairs = mesh.shape["batch"], mesh.shape["chan"]
    rows, width, block = fb.shape[2] // count, fb.shape[3] // pairs, fb.shape[2] // pairs
    banks = fb.shape[0]
    return (
        count == 2 * pairs
        and pairs & (pairs - 1) == 0
        and fi.shape[0] == count
        and fb.shape == cb.shape
        and fi.shape[3] == fb.shape[2]
        and rows % 16 == 0
        and width % 128 == 0
        and block == width
        and all(x.shape[1] ** 2 % block == 0 for x in (fi, ci))
        and 2 * banks <= 128
        and all(x.shape[1] == x.shape[2] and x.shape[1] % 16 == 0 for x in (fi, ci))
    )


def solution(mesh):
    def step(*args):
        body = pair_device if fits_pairs(mesh, *args) else plain_device
        mapped = jax.shard_map(
            body,
            mesh=mesh,
            in_specs=(
                P("batch", None, None, None),
                P("batch", None, None, "chan"),
                P(None, None, "batch", "chan"),
                P(),
                P("batch", None, None, None),
                P("batch", None, None, "chan"),
                P(None, None, "batch", "chan"),
                P(),
            ),
            out_specs=(
                P("batch", None, None, "chan"),
                P(None, None, "batch", "chan"),
                P("batch", None),
                P("batch", None, None, "chan"),
                P(None, None, "batch", "chan"),
                P("batch", None),
            ),
            check_vma=False,
        )
        return mapped(*args)

    return step
```

```python
import functools

import jax
import jax.numpy as jnp
from jax import lax
from jax.experimental import pallas as pl
from jax.experimental.pallas import tpu as pltpu
from jax.sharding import PartitionSpec as P


HIGH = lax.Precision.HIGHEST
F32 = jnp.float32
BF16 = jnp.bfloat16


def shifted(padded, row_shift, col_shift, side):
    window = padded[:, row_shift : row_shift + side, col_shift : col_shift + side, :]
    return window.reshape(window.shape[0], side * side, window.shape[3])


def local_grads(inputs, upstream, kernels, side):
    samples_here = inputs.shape[0]
    pad_in = jnp.pad(inputs, ((0, 0), (1, 1), (1, 1), (0, 0)))
    pad_up = jnp.pad(upstream, ((0, 0), (1, 1), (1, 1), (0, 0)))
    flat_up = upstream.reshape(samples_here, side * side, upstream.shape[3])
    delta = jnp.zeros((samples_here, side * side, inputs.shape[3]), F32)
    grad_taps = []
    for row_shift in range(3):
        for col_shift in range(3):
            tap = 3 * row_shift + col_shift
            window_in = shifted(pad_in, row_shift, col_shift, side)
            window_up = shifted(pad_up, 2 - row_shift, 2 - col_shift, side)
            grad_taps.append(
                jnp.einsum("bpc,bpo->bco", window_in, flat_up, preferred_element_type=F32) / side
            )
            delta = delta + jnp.einsum(
                "bpo,bco->bpc", window_up, kernels[:, tap], preferred_element_type=F32
            )
    return (delta.reshape(samples_here, side, side, inputs.shape[3]), jnp.stack(grad_taps, axis=1))


def plain_layer(inputs, upstream, bank_part, coefs):
    side = inputs.shape[1]
    flat_bank = bank_part.reshape(bank_part.shape[0], -1).astype(F32)
    mixed_all = jnp.dot(coefs, flat_bank, precision=HIGH)
    mixed_all = mixed_all.reshape((coefs.shape[0],) + bank_part.shape[1:]).astype(BF16)
    kernels = lax.all_to_all(mixed_all, "batch", split_axis=0, concat_axis=2, tiled=True)
    delta, kernel_grad = local_grads(inputs, upstream, kernels, side)
    delta_total = lax.psum(delta.astype(BF16), "chan").astype(F32)
    width = delta.shape[3] // lax.axis_size("chan")
    delta_part = lax.dynamic_slice_in_dim(delta_total, lax.axis_index("chan") * width, width, 3)
    moved = lax.all_to_all(
        kernel_grad.astype(BF16), "batch", split_axis=2, concat_axis=0, tiled=True
    ).astype(kernel_grad.dtype)
    flat_grads = moved.reshape(moved.shape[0], -1)
    update = jnp.dot(coefs.T, flat_grads, precision=HIGH).reshape(bank_part.shape)
    dcoef_part = lax.dot_general(flat_grads, flat_bank, (((1,), (1,)), ((), ())), precision=HIGH)
    return (delta_part.astype(BF16), update, dcoef_part)


def plain_logits(coefs, totals, samples_here):
    first_row = lax.axis_index("batch") * samples_here
    own_coefs = lax.dynamic_slice_in_dim(coefs, first_row, samples_here, 0)
    own_totals = lax.dynamic_slice_in_dim(totals, first_row, samples_here, 0)
    return own_coefs * (own_totals - jnp.sum(own_coefs * own_totals, axis=1, keepdims=True))


def plain_device(fi, fu, fb, fc, ci, cu, cb, cc):
    fine_delta, fine_update, fine_partial = plain_layer(fi, fu, fb, fc)
    coarse_delta, coarse_update, coarse_partial = plain_layer(ci, cu, cb, cc)
    fine_total, coarse_total = lax.psum((fine_partial, coarse_partial), ("batch", "chan"))
    fine_logit = plain_logits(fc, fine_total, fi.shape[0])
    coarse_logit = plain_logits(cc, coarse_total, fi.shape[0])
    return (fine_delta, fine_update, fine_logit, coarse_delta, coarse_update, coarse_logit)


def place():
    me = lax.axis_index("batch")
    return me, lax.div(me, 2), lax.rem(me, 2), lax.axis_index("chan")


def smem(n):
    return [pl.BlockSpec(memory_space=pltpu.SMEM) for _ in range(n)]


def hbm(n):
    return [pl.BlockSpec(memory_space=pl.ANY) for _ in range(n)]


def vmem(n):
    return [pl.BlockSpec(memory_space=pltpu.VMEM) for _ in range(n)]


def call(body, out_shapes, in_specs, out_specs, scratch=(), flops=0, nbytes=0, grant=16 * 1024 * 1024):
    return pl.pallas_call(
        body,
        out_shape=out_shapes,
        in_specs=in_specs,
        out_specs=out_specs,
        scratch_shapes=list(scratch),
        compiler_params=pltpu.CompilerParams(vmem_limit_bytes=grant),
        cost_estimate=pl.CostEstimate(flops=flops, bytes_accessed=nbytes, transcendentals=0),
    )


def start(src, dst, sem):
    copy = pltpu.make_async_copy(src, dst, sem)
    copy.start()
    return copy


def fill_windows(up, side, ref):
    pixels, width = up.shape
    wide = up.astype(F32)
    col = lax.rem(lax.broadcasted_iota(jnp.int32, (pixels, width), 0), side)
    zeros = jnp.zeros((side, 3 * width), BF16)
    ref[0:side, :] = zeros
    ref[side + pixels :, :] = zeros
    body = slice(side, side + pixels)
    ref[body, 0:width] = jnp.where(col == side - 1, 0.0, pltpu.roll(wide, pixels - 1, 0)).astype(BF16)
    ref[body, width : 2 * width] = up
    ref[body, 2 * width :] = jnp.where(col == 0, 0.0, pltpu.roll(wide, 1, 0)).astype(BF16)


def window(ref, side, dy):
    first = (2 - dy) * side
    return ref[first : first + ref.shape[0] - 2 * side, :]


def all_windows(ref, side):
    return jnp.concatenate([window(ref, side, dy) for dy in range(3)], axis=1)


def dot_nt(a, b):
    return lax.dot_general(a, b, (((1,), (1,)), ((), ())), preferred_element_type=F32)


def dot_tn(a, b):
    return lax.dot_general(a, b, (((0,), (0,)), ((), ())), preferred_element_type=F32)


def front_body(pairs, side, fx, fup, *rest):
    outs, (v_fx, v_fup, windows, staged, sem_in, sem_out) = rest[:pairs], rest[pairs:]
    _, pair, _, _ = place()
    loads = [start(fup, v_fup, sem_in.at[0]), start(fx, v_fx, sem_in.at[1])]
    loads[0].wait()
    fill_windows(v_fup[...], side, windows)
    loads[1].wait()
    got = dot_tn(v_fx[...], all_windows(windows, side))
    staged[...] = (got * (1.0 / side)).astype(BF16)
    rows = staged.shape[0] // pairs
    stores = []
    for d, out in enumerate(outs):
        first = pl.multiple_of(jnp.bitwise_xor(pair, d) * rows, rows)
        stores.append(start(staged.at[pl.ds(first, rows), :], out, sem_out.at[d]))
    for store in stores:
        store.wait()


def load_banks(own, other, v_banks, sems):
    taps, width = own.shape[1], own.shape[3]
    loads = []
    for t in range(taps):
        lanes = slice(t * width, (t + 1) * width)
        loads.append(
            [
                start(bank.at[:, t], v_banks.at[src, :, :, lanes], sems.at[src, t])
                for src, bank in enumerate((own, other))
            ]
        )
    return loads


def half_row(src, rows):
    _, _, half, _ = place()
    return pl.multiple_of((half if src == 0 else 1 - half) * rows, rows)


def spread(weights, chunk):
    count, terms = len(weights), len(weights[0])
    dims = (chunk, terms * chunk)
    lane = lax.broadcasted_iota(jnp.int32, dims, 1)
    same = lax.broadcasted_iota(jnp.int32, dims, 0) == lax.rem(lane, chunk)
    term = lax.div(lane[0:8], chunk)
    high, low = [], []
    for n in range(count):
        line = jnp.full((8, terms * chunk), weights[n][0], F32)
        for k in range(1, terms):
            line = jnp.where(term == k, weights[n][k], line)
        value = jnp.where(same, jnp.concatenate([line] * (chunk // 8), axis=0), 0.0)
        rounded = value.astype(BF16)
        high.append(rounded)
        low.append((value - rounded.astype(F32)).astype(BF16))
    return jnp.concatenate(high + low, axis=0)


def dot_nn(a, b):
    return lax.dot_general(a, b, (((1,), (0,)), ((), ())), preferred_element_type=F32)


def chunk_of(rows, terms):
    return max(16, min(rows, 256 // terms))


def mix_weights(pairs, coefs):
    me, _, _, _ = place()
    banks = coefs.shape[1]
    return [[coefs[jnp.bitwise_xor(me, 2 * d), k] for k in range(banks)] for d in range(pairs)]


def pack_body(pairs, cx, cup, *rest):
    packs, (v_x, v_up, sem_in, sem_out) = rest[:pairs], rest[pairs:]
    _, pair, _, _ = place()
    pixels, width = v_up.shape
    loads = [start(cup, v_up, sem_in.at[0]), start(cx, v_x, sem_in.at[1])]
    loads[0].wait()
    stores = [start(v_up, out.at[0:pixels, :], sem_out.at[0, d]) for d, out in enumerate(packs)]
    loads[1].wait()
    for d, out in enumerate(packs):
        first = pl.multiple_of(jnp.bitwise_xor(pair, d) * width, width)
        stores.append(start(v_x.at[:, pl.ds(first, width)], out.at[pixels:, :], sem_out.at[1, d]))
    for store in stores:
        store.wait()


def tables_body(pairs, chunk, fine_coefs, coarse_coefs, *tables):
    me, _, _, _ = place()
    samples = 2 * pairs
    for n, coefs in enumerate((fine_coefs, coarse_coefs)):
        banks = coefs.shape[1]
        to_updates, row = tables[2 * n : 2 * n + 2]
        weights = [[coefs[jnp.bitwise_xor(me, d), k] for d in range(samples)] for k in range(banks)]
        to_updates[...] = spread(weights, chunk)
        lane = lax.broadcasted_iota(jnp.int32, row.shape, 1)
        line = jnp.zeros(row.shape, F32)
        for k in range(banks):
            line = jnp.where(lane == k, coefs[me, k], line)
        row[...] = line


def mix_lanes(pairs, table, v_banks, staged, lanes):
    _, banks, rows, _ = v_banks.shape
    chunk = table.shape[1] // banks
    for src in range(2):
        base = half_row(src, rows)
        for at in range(0, rows, chunk):
            right = v_banks[src, :, at : at + chunk, lanes]
            got = dot_nn(table, right.reshape(banks * chunk, right.shape[2]))
            got = (got[: pairs * chunk] + got[pairs * chunk :]).astype(BF16)
            into = pl.ds(pl.multiple_of(base + at, 16), chunk)
            for d in range(pairs):
                staged[d, into, lanes] = got[d * chunk : (d + 1) * chunk]


def mix_body(pairs, coefs, own, other, *rest):
    outs, (s_coefs, v_banks, staged, sem_coefs, sem_in, sem_out) = rest[:pairs], rest[pairs:]
    taps, width = own.shape[1], own.shape[3]
    first = start(coefs, s_coefs, sem_coefs)
    loads = load_banks(own, other, v_banks, sem_in)
    first.wait()
    table = spread(mix_weights(pairs, s_coefs), chunk_of(own.shape[2], own.shape[0]))
    stores = []
    for t in range(0, taps, 4):
        for some in loads[t : t + 4]:
            for load in some:
                load.wait()
        lanes = slice(t * width, min(t + 4, taps) * width)
        mix_lanes(pairs, table, v_banks, staged, lanes)
        for d, out in enumerate(outs):
            stores.append(start(staged.at[d, :, lanes], out.at[:, lanes], sem_out.at[d, t]))
    for store in stores:
        store.wait()


def delta_body(pairs, side, up, *rest):
    mixed, outs = rest[:pairs], rest[pairs : 2 * pairs]
    v_up, windows, kernels, staged, sem_in, sem_out = rest[2 * pairs :]
    _, pair, _, chan = place()
    rows = kernels.shape[0] // pairs
    first_load = start(up, v_up, sem_in.at[pairs])
    loads = []
    for d in range(pairs):
        slot = jnp.bitwise_xor(jnp.bitwise_xor(pair, d), chan)
        at = pl.multiple_of(slot * rows, rows)
        loads.append(start(mixed[d], kernels.at[pl.ds(at, rows), :], sem_in.at[d]))
    first_load.wait()
    fill_windows(v_up[...], side, windows)
    for load in loads:
        load.wait()
    stores = []
    got = dot_nt(all_windows(windows, side), kernels[...])
    for slot in range(pairs):
        staged[slot] = got[:, slot * rows : (slot + 1) * rows].astype(BF16)
        stores.append(start(staged.at[slot], outs[slot], sem_out.at[slot]))
    for store in stores:
        store.wait()


def dcoef_rows(pairs, grads, v_banks, lane0):
    _, banks, rows, span = v_banks.shape
    chunk = chunk_of(rows, banks)
    cross = None
    for src in range(2):
        for at in range(0, rows, chunk):
            first = pl.multiple_of(half_row(src, rows) + at, 16)
            left = grads[:, pl.ds(first, chunk), :].reshape(pairs * chunk, span)
            right = v_banks[src, :, at : at + chunk, :].reshape(banks * chunk, span)
            one = dot_nt(left, right)
            cross = one if cross is None else cross + one
    row = lax.rem(lax.broadcasted_iota(jnp.int32, cross.shape, 0), chunk)
    col = lax.rem(lax.broadcasted_iota(jnp.int32, cross.shape, 1), chunk)
    kept = jnp.where(row == col, cross, 0.0)
    kept = jnp.sum(kept.reshape(pairs, chunk, banks * chunk), axis=1)
    bank_of = lax.div(lax.broadcasted_iota(jnp.int32, kept.shape, 1), chunk)
    lane = lax.broadcasted_iota(jnp.int32, (pairs, 128), 1)
    total = jnp.zeros((pairs, 128), F32)
    for k in range(banks):
        one = jnp.sum(jnp.where(bank_of == k, kept, 0.0), axis=1, keepdims=True)
        total = jnp.where(lane == lane0 + k, one, total)
    return total


def coarse_body(pairs, side, coefs, own, other, *rest):
    ups, parts, rest = rest[:pairs], rest[pairs : 2 * pairs], rest[2 * pairs :]
    s_coefs, v_banks, v_mixed, v_ups, windows, v_parts, sem_coefs, sem_bank, sem_in, sem_out = rest
    taps, width = own.shape[1], own.shape[3]
    pixels = side * side
    first = start(coefs, s_coefs, sem_coefs)
    loads = [start(ups[d].at[0:pixels, :], v_ups.at[d], sem_in.at[d]) for d in range(pairs)]
    bank_loads = load_banks(own, other, v_banks, sem_bank)
    first.wait()
    table = spread(mix_weights(pairs, s_coefs), chunk_of(own.shape[2], own.shape[0]))
    for t in range(0, taps, 4):
        for some in bank_loads[t : t + 4]:
            for load in some:
                load.wait()
        mix_lanes(pairs, table, v_banks, v_mixed, slice(t * width, min(t + 4, taps) * width))
    stores = []
    third = windows.shape[1]
    for d in range(pairs):
        loads[d].wait()
        fill_windows(v_ups[d], side, windows)
        part = None
        for dy in range(3):
            one = dot_nt(window(windows, side, dy), v_mixed[d, :, dy * third : (dy + 1) * third])
            part = one if part is None else part + one
        v_parts[d] = part.astype(BF16)
        stores.append(start(v_parts.at[d], parts[d], sem_out.at[d]))
    for store in stores:
        store.wait()


def calm_body(pairs, side, own, other, *rest):
    bufs, grads, table, rest = rest[:pairs], rest[pairs : 2 * pairs], rest[2 * pairs], rest[2 * pairs + 1 :]
    v_banks, v_bufs, windows, v_grads, sem_bank, sem_in, sem_out = rest
    pixels = side * side
    loads = [start(bufs[d], v_bufs.at[d], sem_in.at[d]) for d in range(pairs)]
    bank_loads = load_banks(own, other, v_banks, sem_bank)
    stores = []
    for d in range(pairs):
        loads[d].wait()
        fill_windows(v_bufs[d, 0:pixels, :], side, windows)
        got = dot_tn(v_bufs[d, pixels:, :], all_windows(windows, side))
        v_grads[d] = (got * (1.0 / side)).astype(BF16)
        stores.append(start(v_grads.at[d], grads[d], sem_out.at[d]))
    for some in bank_loads:
        for load in some:
            load.wait()
    table[...] = dcoef_rows(pairs, v_grads, v_banks, own.shape[0])
    for store in stores:
        store.wait()


def as_pair(rows):
    high = rows.astype(BF16)
    return jnp.concatenate([high, (rows - high.astype(F32)).astype(BF16)], axis=0)


def from_pair(both):
    wide = both.astype(F32)
    return wide[0:8] + wide[8:16]


def late_body(pairs, own, other, more, *rest):
    gots, parts, outs = rest[:pairs], rest[pairs : 2 * pairs - 1], rest[2 * pairs - 1 : 3 * pairs - 2]
    mine, v_banks, v_gots, v_out, sem_bank, sem_in, sem_part, sem_out = rest[3 * pairs - 2 :]
    loads = [[start(gots[d], v_gots.at[d], sem_in.at[d]) for d in range(pairs)]]
    loads += load_banks(own, other, v_banks, sem_bank)
    pixels = parts[0].shape[0]
    loads.append(
        [start(parts[d], v_out.at[d, 0:pixels, :], sem_part.at[d]) for d in range(pairs - 1)]
    )
    for some in loads:
        for load in some:
            load.wait()
    total = dcoef_rows(pairs, v_gots, v_banks, 0) + more[...]
    mine[...] = jnp.broadcast_to(total[0:1], mine.shape)
    stores = []
    for d in range(pairs - 1):
        v_out[d, pixels:, :] = as_pair(jnp.broadcast_to(total[d + 1 : d + 2], mine.shape))
        stores.append(start(v_out.at[d], outs[d], sem_out.at[d]))
    for store in stores:
        store.wait()


def slot_body(pairs, first_part, first_row, *rest):
    gots, slots, rest = rest[: pairs - 1], rest[pairs - 1 : 2 * pairs - 1], rest[2 * pairs - 1 :]
    mine, v_slots, sem_in, sem_out = rest
    _, pair, _, chan = place()
    pixels = first_part.shape[0]
    loads, at = [], []
    for d in range(pairs):
        slot = jnp.bitwise_xor(jnp.bitwise_xor(pair, d), chan)
        at.append(slot)
        if d == 0:
            loads.append(start(first_part, v_slots.at[slot, 0:pixels, :], sem_in.at[0]))
        else:
            loads.append(start(gots[d - 1], v_slots.at[slot], sem_in.at[d]))
    for load in loads:
        load.wait()
    total = first_row[...]
    for d in range(1, pairs):
        total = total + from_pair(v_slots[at[d], pixels:, :])
    both = as_pair(total)
    mine[...] = from_pair(both)
    for s in range(pairs):
        v_slots[s, pixels:, :] = both
    stores = [start(v_slots.at[s], slots[s], sem_out.at[s]) for s in range(pairs)]
    for store in stores:
        store.wait()


def update_body(pairs, layers, *rest):
    samples = 2 * pairs
    tables, rest = rest[:layers], rest[layers:]
    all_gots, rest = rest[: layers * samples], rest[layers * samples :]
    updates, (v_grads, staged, sem_in, sem_out) = rest[:layers], rest[layers:]
    _, _, half, _ = place()
    banks, taps, rows, width = updates[0].shape
    first = pl.multiple_of(half * rows, rows)
    loads = []
    for n in range(layers):
        gots = all_gots[n * samples : (n + 1) * samples]
        for d in range(samples):
            src = gots[d % 2 * pairs + d // 2].at[pl.ds(first, rows), 0 : taps * width]
            loads.append(start(src, v_grads.at[n, d], sem_in.at[n, d]))
    for load in loads:
        load.wait()
    chunk = chunk_of(rows, samples)
    stores = []
    for n in range(layers):
        table = tables[n][...]
        half_table = banks * chunk
        for at in range(0, rows, chunk):
            right = v_grads[n, :, at : at + chunk, :].reshape(samples * chunk, taps * width)
            got = dot_nn(table, right)
            got = got[:half_table] + got[half_table:]
            for k in range(banks):
                for t in range(taps):
                    staged[n, k, t, at : at + chunk, :] = got[
                        k * chunk : (k + 1) * chunk, t * width : (t + 1) * width
                    ]
            some = slice(at, at + chunk)
            stores.append(
                start(staged.at[n, :, :, some], updates[n].at[:, :, some], sem_out.at[n, at // chunk])
            )
    for store in stores:
        store.wait()


def sum_body(pairs, *rest):
    pieces, (out, held, sem_in, sem_out) = rest[:pairs], rest[pairs:]
    loads = [start(pieces[d], held.at[d], sem_in.at[d]) for d in range(pairs)]
    for load in loads:
        load.wait()
    total = held[0].astype(F32)
    for d in range(1, pairs):
        total = total + held[d].astype(F32)
    held[pairs] = total.astype(BF16)
    start(held.at[pairs], out, sem_out).wait()


def final_body(pairs, banks, mine, fine_row, coarse_row, *rest):
    pieces, (fine_out, coarse_out, out, held, sem_in, sem_out) = rest[:pairs], rest[pairs:]
    loads = [start(pieces[d], held.at[d], sem_in.at[d]) for d in range(pairs)]
    for load in loads:
        load.wait()
    pixels = out.shape[0]
    total = held[0, 0:pixels, :].astype(F32)
    for d in range(1, pairs):
        total = total + held[d, 0:pixels, :].astype(F32)
    held[pairs, 0:pixels, :] = total.astype(BF16)
    store = start(held.at[pairs, 0:pixels, :], out, sem_out)
    total = mine[...]
    for d in range(1, pairs):
        total = total + from_pair(held[d, pixels:, :])
    for lane0, row, logit in ((0, fine_row, fine_out), (banks, coarse_row, coarse_out)):
        own = row[:, 0:banks]
        some = total[0:1, lane0 : lane0 + banks]
        logit[...] = own * (some - jnp.sum(own * some, axis=1, keepdims=True))
    store.wait()


def shape(*dims, dtype=BF16):
    return jax.ShapeDtypeStruct(dims, dtype)


def pair_device(fi, fu, fb, fc, ci, cu, cb, cc):
    return pair_steps(fi, fu, fb, fc, ci, cu, cb, cc)


def pair_steps(fi, fu, fb, fc, ci, cu, cb, cc):
    pairs = lax.axis_size("chan")
    count = lax.axis_size("batch")
    fine_side, coarse_side = fi.shape[1], ci.shape[1]
    fine_px, coarse_px = fine_side**2, coarse_side**2
    channels = fi.shape[3]
    banks, taps, rows, width = fb.shape
    block = 2 * rows
    span = taps * width
    fx, fup = fi.reshape(fine_px, channels), fu.reshape(fine_px, width)
    cx, cup = ci.reshape(coarse_px, channels), cu.reshape(coarse_px, width)

    def over_batch(x, d):
        return lax.ppermute(x, "batch", [(i, i ^ d) for i in range(count)])

    def over_chan(x, d):
        return lax.ppermute(x, "chan", [(i, i ^ d) for i in range(pairs)])

    def send(move, pieces, distances):
        out = []
        for piece, d in zip(pieces, distances):
            out.append(move(piece, d))
        return out

    def to_pairs(pieces):
        moved = send(lambda x, d: over_batch(x, 2 * d), pieces[1:], range(1, pairs))
        return [pieces[0]] + moved

    dma = pltpu.SemaphoreType.DMA
    work = 2 * fine_px * channels * span
    bank_bytes = 2 * banks * rows * span

    other_fb, other_cb = send(lambda x, d: over_batch(x, 1), (fb, cb), range(2))

    def mix_scratch():
        return [pltpu.SMEM(fc.shape, F32), pltpu.VMEM((2, banks, rows, span), BF16), pltpu.VMEM((pairs, block, span), BF16)]

    packs = call(
        functools.partial(pack_body, pairs),
        [shape(2 * coarse_px, block)] * pairs, hbm(2), hbm(pairs),
        [
            pltpu.VMEM((coarse_px, channels), BF16), pltpu.VMEM((coarse_px, width), BF16),
            dma((2,)), dma((2, pairs)),
        ],
        nbytes=bank_bytes, grant=67043328,
    )(cx, cup)
    bufs = to_pairs(packs)
    chunk = chunk_of(rows, count)
    fine_table, fine_row, coarse_table, coarse_row = call(
        functools.partial(tables_body, pairs, chunk),
        [shape(2 * banks * chunk, count * chunk), shape(1, 128, dtype=F32)] * 2,
        smem(2), vmem(4), flops=work, nbytes=bank_bytes,
    )(fc, cc)

    mixed = call(
        functools.partial(mix_body, pairs),
        [shape(block, span)] * pairs, hbm(3), hbm(pairs),
        mix_scratch() + [dma, dma((2, taps)), dma((pairs, taps))],
        flops=4 * banks * pairs * block * span, nbytes=3 * bank_bytes, grant=65500000,
    )(fc, fb, other_fb)
    mixed = to_pairs(mixed)

    parts = call(
        functools.partial(coarse_body, pairs, coarse_side),
        [shape(coarse_px, block)] * pairs, hbm(3 + pairs), hbm(pairs),
        mix_scratch() + [
            pltpu.VMEM((pairs, coarse_px, width), BF16),
            pltpu.VMEM((coarse_px + 2 * coarse_side, 3 * width), BF16),
            pltpu.VMEM((pairs, coarse_px, block), BF16),
            dma, dma((2, taps)), dma((pairs,)), dma((pairs,)),
        ],
        flops=work, nbytes=3 * bank_bytes,
    )(cc, cb, other_cb, *bufs)

    front = call(
        functools.partial(front_body, pairs, fine_side),
        [shape(block, span)] * pairs, hbm(2), hbm(pairs),
        [
            pltpu.VMEM((fine_px, channels), BF16), pltpu.VMEM((fine_px, width), BF16),
            pltpu.VMEM((fine_px + 2 * fine_side, 3 * width), BF16), pltpu.VMEM((channels, span), BF16),
            dma((2,)), dma((pairs,)),
        ],
        flops=work, nbytes=5 * fine_px * channels,
    )(fx, fup)
    fine_own = to_pairs(front)

    fine_parts = call(
        functools.partial(delta_body, pairs, fine_side),
        [shape(fine_px, block)] * pairs, hbm(1 + pairs), hbm(pairs),
        [
            pltpu.VMEM((fine_px, width), BF16),
            pltpu.VMEM((fine_px + 2 * fine_side, 3 * width), BF16),
            pltpu.VMEM((channels, span), BF16), pltpu.VMEM((pairs, fine_px, block), BF16),
            dma((pairs + 1,)), dma((pairs,)),
        ],
        flops=work, nbytes=5 * fine_px * channels,
    )(fup, *mixed)
    fine_parts = [fine_parts[0]] + send(over_chan, fine_parts[1:], range(1, pairs))

    tile = shape(8, 128, dtype=F32)
    loaded = [shape(coarse_px + 16, block)]
    calm = call(
        functools.partial(calm_body, pairs, coarse_side),
        [shape(block, span)] * pairs + [shape(pairs, 128, dtype=F32)],
        hbm(2 + pairs), hbm(pairs) + vmem(1),
        [
            pltpu.VMEM((2, banks, rows, span), BF16), pltpu.VMEM((pairs, 2 * coarse_px, block), BF16),
            pltpu.VMEM((coarse_px + 2 * coarse_side, 3 * width), BF16),
            pltpu.VMEM((pairs, block, span), BF16),
            dma((2, taps)), dma((pairs,)), dma((pairs,)),
        ],
        flops=work, nbytes=3 * bank_bytes,
    )(cb, other_cb, *bufs)
    coarse_own, coarse_dcoef = calm[:pairs], calm[pairs]

    late = call(
        functools.partial(late_body, pairs),
        loaded * (pairs - 1) + [tile],
        hbm(2) + vmem(1) + hbm(2 * pairs - 1), hbm(pairs - 1) + vmem(1),
        [
            pltpu.VMEM((2, banks, rows, span), BF16), pltpu.VMEM((pairs, block, span), BF16),
            pltpu.VMEM((pairs - 1, coarse_px + 16, block), BF16),
            dma((2, taps)), dma((pairs,)), dma((pairs - 1,)), dma((pairs - 1,)),
        ],
        flops=work, nbytes=3 * bank_bytes,
    )(fb, other_fb, coarse_dcoef, *fine_own, *parts[1:])
    tiles = send(lambda x, d: over_batch(x, 2 * d), late[: pairs - 1], range(1, pairs))

    slots = call(
        functools.partial(slot_body, pairs),
        loaded * pairs + [tile],
        hbm(1) + vmem(1) + hbm(pairs - 1), hbm(pairs) + vmem(1),
        [pltpu.VMEM((pairs, coarse_px + 16, block), BF16), dma((pairs,)), dma((pairs,))],
        nbytes=4 * pairs * coarse_px * block,
    )(parts[0], late[pairs - 1], *tiles)
    slots, mine = slots[:pairs], slots[pairs]
    slots = [slots[0]] + send(over_chan, slots[1:], range(1, pairs))

    swapped = [
        send(lambda x, d: over_batch(x, 1), own, range(pairs))
        for own in (fine_own, coarse_own)
    ]

    def update(table, own, others):
        return call(
            functools.partial(update_body, pairs, 1),
            [shape(banks, taps, rows, width, dtype=F32)], vmem(1) + hbm(2 * pairs), hbm(1),
            [
                pltpu.VMEM((1, count, rows, span), BF16),
                pltpu.VMEM((1, banks, taps, rows, width), F32),
                dma((1, count)), dma((1, taps)),
            ],
            flops=2 * banks * count * rows * span, nbytes=3 * bank_bytes,
        )(table, *own, *others)[0]

    fine_update = update(fine_table, fine_own, swapped[0])
    coarse_update = update(coarse_table, coarse_own, swapped[1])

    fine_delta = call(
        functools.partial(sum_body, pairs),
        shape(fine_px, block), hbm(pairs), hbm(1)[0],
        [pltpu.VMEM((pairs + 1, fine_px, block), BF16), dma((pairs,)), dma],
        nbytes=2 * fine_px * channels,
    )(*fine_parts)
    fine_logit, coarse_logit, coarse_delta = call(
        functools.partial(final_body, pairs, banks),
        [shape(1, banks, dtype=F32)] * 2 + [shape(coarse_px, block)],
        vmem(3) + hbm(pairs), vmem(2) + hbm(1),
        [pltpu.VMEM((pairs + 1, coarse_px + 16, block), BF16), dma((pairs,)), dma],
        nbytes=2 * coarse_px * channels,
    )(mine, fine_row, coarse_row, *slots)
    fine_delta = fine_delta.reshape(1, fine_side, fine_side, block)
    coarse_delta = coarse_delta.reshape(1, coarse_side, coarse_side, block)
    return (fine_delta, fine_update, fine_logit, coarse_delta, coarse_update, coarse_logit)


def fits_pairs(mesh, fi, fu, fb, fc, ci, cu, cb, cc):
    count, pairs = mesh.shape["batch"], mesh.shape["chan"]
    rows, width, block = fb.shape[2] // count, fb.shape[3] // pairs, fb.shape[2] // pairs
    banks = fb.shape[0]
    return (
        count == 2 * pairs
        and pairs & (pairs - 1) == 0
        and fi.shape[0] == count
        and fb.shape == cb.shape
        and fi.shape[3] == fb.shape[2]
        and rows % 16 == 0
        and width % 128 == 0
        and block == width
        and all(x.shape[1] ** 2 % block == 0 for x in (fi, ci))
        and 2 * banks <= 128
        and all(x.shape[1] == x.shape[2] and x.shape[1] % 16 == 0 for x in (fi, ci))
    )


def solution(mesh):
    def step(*args):
        body = pair_device if fits_pairs(mesh, *args) else plain_device
        mapped = jax.shard_map(
            body,
            mesh=mesh,
            in_specs=(
                P("batch", None, None, None),
                P("batch", None, None, "chan"),
                P(None, None, "batch", "chan"),
                P(),
                P("batch", None, None, None),
                P("batch", None, None, "chan"),
                P(None, None, "batch", "chan"),
                P(),
            ),
            out_specs=(
                P("batch", None, None, "chan"),
                P(None, None, "batch", "chan"),
                P("batch", None),
                P("batch", None, None, "chan"),
                P(None, None, "batch", "chan"),
                P("batch", None),
            ),
            check_vma=False,
        )
        return mapped(*args)

    return step
```
